32 devices in a mesh: row: 8 (over z, y), col: 4 (over x, core).
Axes of the slice: x: 2, y: 2, z: 4, core: 2. Of those that a mesh axis runs over, the one named last changes fastest.
Arguments:
- three_index: bfloat16 [8, 4, 8, 2, 128, 128], P('row', 'col'), may hold values from -6 to 6
- slot_pair: int32 [8, 4, 8], P('row', 'col'), may hold values from -1 to 31, as said below
- coeff: bfloat16 [4096, 256], P(('col', 'row')), may hold values from -0.125 to 0.125
- occ_mask: int32 [32, 2], P('col'), may hold values 0 or 1
Outputs:
- exchange_block: bfloat16 [4096, 4096], P('row', 'col')
The draws below stay inside these ranges and needn't reach their ends.
Inputs may be any that keep to these rules, and one draw needn't show every extreme that they name: `slot_pair`: on each device (first two dimensions) the 8 slots name distinct local pair blocks mb * 8 + nb, the live ones first and -1 after them; in every draw some device fills all 8 slots.
All inputs are finite; a program needn't handle non-finite values. No bound on the sum of `occ_mask` on one device may be relied on, other than what follows from the above.
Results may differ from the reference program's by a relative error of at most 0.0057.
Values may be sent and summed in bfloat16 or wider, within the bound.
No kernel may reach another device: no remote copies, remote signals or barrier semaphores. Data moves between devices by JAX's collectives and lax.ppermute only.
A program may use at most 64 MiB of HBM per device.

```python
import jax
import jax.numpy as jnp
from jax import lax

BLK = 128
MB_DEV = 4
AUX = 2
OCC = 256
KB = 8
NAO = 4096
NB = 32
NBC = 8
NOB = 2
N_ROW = 8
N_COL = 4


def draw_slot_pair(key, part):
    npairs = MB_DEV * NBC
    total = N_ROW * N_COL
    first, second, third, fourth = jax.random.split(key, 4)
    base = jax.random.randint(first, (total,), 1, 4)
    heavy = jax.random.randint(second, (total,), 0, 8) == 0
    counts = jnp.where(heavy, KB, jnp.minimum(base, KB))
    chosen = jax.random.randint(third, (), 0, total)
    counts = counts.at[chosen].set(KB)
    orders = jax.vmap(lambda sub: jax.random.permutation(sub, npairs))(jax.random.split(fourth, total))[:, :KB]
    positions = jnp.arange(KB)[None, :]
    result = jnp.where(positions < counts[:, None], orders, -1)
    return result.reshape(N_ROW, N_COL, KB).astype(jnp.int32)


def with_ends(drawn, rng, least, top_value):
    extent = drawn.shape
    index_at = [jax.random.randint(jax.random.fold_in(rng, axis), (), 0, extent[axis]) for axis in range(len(extent))]
    drawn = drawn.at[tuple(index_at)].set(least)
    longest = extent.index(max(extent))
    index_at[longest] = (index_at[longest] + 1) % extent[longest]
    return drawn.at[tuple(index_at)].set(top_value)


def level_of(rng, dims, pieces, least, largest):
    gain = 1.0
    for dim, parts in pieces:
        draws = jax.random.uniform(jax.random.fold_in(jax.random.fold_in(rng, 6), dim), (parts,), jnp.float32, least / len(pieces), largest / len(pieces))
        gain = gain * jnp.repeat(jnp.exp(draws), dims[dim] // parts).reshape((-1,) + (1,) * (len(dims) - 1 - dim))
    return gain


def bell_draw(key, shape, scale, bound, cuts=(), kind=jnp.bfloat16):
    entries = jax.random.normal(key, shape, jnp.float32) * scale
    if len(cuts) > 0:
        entries = level_of(key, shape, cuts, -0.22, 0.18) * entries
    return jnp.clip(entries, min=-bound, max=bound).astype(kind)


def setup_inputs(seed: int = 0) -> dict:
    keys = jax.random.split(jax.random.key(seed), 5)
    three_index = bell_draw(keys[0], (N_ROW, N_COL, KB, AUX, BLK, BLK), 1.0, 6.0, ((0, 8), (1, 4)))
    slot_pair = draw_slot_pair(jax.random.fold_in(keys[4], 71), 0)
    coeff = bell_draw(keys[2], (NAO, OCC), (BLK * 16) ** -0.5, 0.125, ((0, 32),))
    occ_mask = with_ends((jax.random.randint(keys[3], (NB, NOB), 0, 3) < 2).astype(jnp.int32), jax.random.fold_in(keys[3], 1), 0, 1)
    return {"three_index": three_index, "slot_pair": slot_pair, "coeff": coeff, "occ_mask": occ_mask}


def reference(three_index, slot_pair, coeff, occ_mask):
    keep = occ_mask.astype(coeff.dtype)[:, None, :, None]
    masked = (coeff.reshape(NB, BLK, NOB, BLK) * keep).reshape(NAO, OCC)
    blocks = three_index.reshape(N_ROW * N_COL * KB, AUX, BLK, BLK)
    slots = slot_pair.reshape(N_ROW * N_COL * KB)

    def add_slot(index, half):
        device = index // KB
        row_index = device // N_COL
        col_index = device % N_COL
        pair = slots[index]
        live = (pair >= 0).astype(half.dtype)
        pair = jnp.maximum(pair, 0)
        mu_start = ((row_index * MB_DEV + pair // NBC) * BLK).astype(jnp.int32)
        nu_start = ((col_index * NBC + pair % NBC) * BLK).astype(jnp.int32)
        rows = lax.dynamic_slice_in_dim(masked, nu_start, BLK, 0).astype(half.dtype)
        block = blocks[index].astype(half.dtype)
        term = jnp.einsum('pab,bi->api', block, rows)
        current = lax.dynamic_slice_in_dim(half, mu_start, BLK, 0)
        return lax.dynamic_update_slice_in_dim(half, current + live * term, mu_start, 0)
    half = jnp.zeros((NAO, AUX, OCC), jnp.float32)
    half = lax.fori_loop(0, N_ROW * N_COL * KB, add_slot, half)
    flat = half.astype(jnp.bfloat16).reshape(NAO, AUX * OCC)
    product = jnp.dot(flat, flat.T, preferred_element_type=jnp.float32)
    return (product / jnp.sqrt(jnp.float32(AUX * OCC))).astype(jnp.bfloat16)
```

```python
import functools
import math

import jax
import jax.numpy as jnp
from jax import lax
from jax.experimental import pallas as pl
from jax.experimental.pallas import tpu as pltpu
from jax.sharding import PartitionSpec as P

MB_DEV = 4
VMEM = pl.BlockSpec(memory_space=pltpu.VMEM)
SMEM = pl.BlockSpec(memory_space=pltpu.SMEM)


class Layout:
    def __init__(self, n_row, n_col, mu_rows):
        self.n_row, self.n_col = n_row, n_col
        self.ratio = n_row // n_col
        self.mu_rows = mu_rows
        self.piece = mu_rows // n_col

    def permute(self, value, target):
        pairs = []
        for row in range(self.n_row):
            for col in range(self.n_col):
                plane, side, place = target(row // self.ratio, row % self.ratio, col)
                pairs.append((row * self.n_col + col, (plane * self.ratio + side) * self.n_col + place))
        return lax.ppermute(value, ("row", "col"), pairs)

    def shift(self, value, plane_bits, side_bits, col_bits):
        return self.permute(value, lambda z, y, w: (z ^ plane_bits, y ^ side_bits, w ^ col_bits))

    def offset(self, quarter):
        return (quarter % 2) * (self.mu_rows // 2) + (quarter // 2) * self.piece


def half_kernel(nu_blocks, block, place_ref, slot_ref, mask_ref, block_ref, *refs):
    pieces, (mine_ref, other_ref, rows_ref) = refs[:-3], refs[-3:]
    rows = pieces[0].shape[0]
    aux, occ = block_ref.shape[1], pieces[0].shape[1]
    half_blocks = mine_ref.shape[0] // block
    for index, piece in enumerate(pieces):
        start = pl.multiple_of(place_ref[1 + index] * rows, rows)
        nu_block = start // block
        for part in range(occ // block):
            columns = slice(part * block, (part + 1) * block)
            value = piece[:, columns]
            kept = jnp.where(mask_ref[nu_block, part] != 0, value, jnp.zeros_like(value))
            rows_ref[pl.ds(start, rows), columns] = kept
    mine_ref[...] = jnp.zeros_like(mine_ref)
    other_ref[...] = jnp.zeros_like(other_ref)

    def add(out_ref, slot, mu_block, nu_block):
        out_rows = pl.ds(pl.multiple_of(mu_block * block, block), block)
        nu_rows = rows_ref[pl.ds(pl.multiple_of(nu_block * block, block), block), :]
        for p in range(aux):
            columns = slice(p * occ, (p + 1) * occ)
            out_ref[out_rows, columns] += jnp.dot(
                block_ref[slot, p], nu_rows, preferred_element_type=jnp.float32
            )

    @pl.loop(0, block_ref.shape[0])
    def _(slot):
        pair = slot_ref[slot]
        mu_block = pair // nu_blocks
        nu_block = pair % nu_blocks
        core = mu_block // half_blocks

        @pl.when((pair >= 0) & (core == place_ref[0]))
        def _():
            add(mine_ref, slot, mu_block - core * half_blocks, nu_block)

        @pl.when((pair >= 0) & (core != place_ref[0]))
        def _():
            add(other_ref, slot, mu_block - core * half_blocks, nu_block)


def split_kernel(place_ref, mine_ref, other_ref, *outs):
    rows = outs[0].shape[0]
    for index, out in enumerate(outs):
        part = pl.ds(pl.multiple_of((place_ref[0] ^ index) * rows, rows), rows)
        out[...] = mine_ref[part, :] + other_ref[part, :]


def product_kernel(n_left, scale, place_ref, *refs):
    left, right, (out_ref, left_rows, right_rows) = refs[:n_left], refs[n_left:-3], refs[-3:]
    rows = left[0].shape[0]
    for index, piece in enumerate(left):
        left_rows[pl.ds(pl.multiple_of(place_ref[index], rows), rows), :] = piece[...]
    for index, piece in enumerate(right):
        right_rows[pl.ds(pl.multiple_of(place_ref[n_left + index], rows), rows), :] = piece[...]
    step = math.gcd(right_rows.shape[0], 256)
    for start in range(0, right_rows.shape[0], step):
        value = lax.dot_general(
            left_rows[...],
            right_rows[start : start + step, :],
            (((1,), (1,)), ((), ())),
            preferred_element_type=jnp.float32,
        )
        out_ref[:, start : start + step] = (value * scale).astype(out_ref.dtype)


def body(three_index, slot_pair, coeff, occ_mask):
    kept_slots, aux, block = three_index.shape[2:5]
    occ = coeff.shape[1]
    n_row, n_col = lax.axis_size("row"), lax.axis_size("col")
    lay = Layout(n_row, n_col, coeff.shape[0] * n_col)
    mu_rows, ratio, width = lay.mu_rows, lay.ratio, aux * occ
    nu_blocks = coeff.shape[0] * n_row // block
    row, col = lax.axis_index("row"), lax.axis_index("col")
    plane, side = row // ratio, row % ratio

    pieces, places = [], []
    for d in range(n_col):
        here = lay.shift(coeff, d, 0, 0) if d else coeff
        for t in range(ratio):
            pieces.append(lay.shift(here, 0, t, 0) if t else here)
            places.append((plane ^ d) * ratio + (side ^ t))

    half = jax.ShapeDtypeStruct((mu_rows // 2, width), jnp.float32)
    mine, other = pl.pallas_call(
        functools.partial(half_kernel, nu_blocks, block),
        out_shape=(half, half),
        in_specs=[SMEM, SMEM, SMEM, VMEM] + [VMEM] * len(pieces),
        out_specs=(VMEM, VMEM),
        scratch_shapes=[pltpu.VMEM((nu_blocks * block, occ), coeff.dtype)],
    )(
        jnp.stack([col % 2] + places),
        slot_pair.reshape(kept_slots),
        occ_mask,
        three_index.reshape(kept_slots, aux, block, block),
        *pieces,
    )

    other = lay.shift(other, 0, 0, 1)
    chips = n_col // 2
    part = jax.ShapeDtypeStruct((lay.piece, width), jnp.float32)
    parts = pl.pallas_call(
        split_kernel,
        out_shape=(part,) * chips,
        in_specs=[SMEM, VMEM, VMEM],
        out_specs=(VMEM,) * chips,
    )((col // 2).reshape(1), mine, other)
    total = parts[0]
    for e in range(1, chips):
        total = total + lay.shift(parts[e], 0, 0, 2 * e)
    final = total.astype(jnp.bfloat16)

    left, places = [], []
    for e in range(chips):
        here = lay.shift(final, 0, 0, 2 * e) if e else final
        for k in range(2):
            left.append(lay.shift(here, 0, 0, 1) if k else here)
            places.append(lay.offset(col ^ (2 * e + k)))
    right = []
    for j in range(n_col):
        here = lay.permute(final, lambda z, y, w: (w ^ j, y, z))
        for t in range(ratio):
            right.append(lay.shift(here, 0, t, 0) if t else here)
            places.append((side ^ t) * mu_rows + lay.offset(plane ^ j))
    return pl.pallas_call(
        functools.partial(product_kernel, len(left), 1.0 / math.sqrt(width)),
        out_shape=jax.ShapeDtypeStruct((mu_rows, ratio * mu_rows), jnp.bfloat16),
        in_specs=[SMEM] + [VMEM] * (len(left) + len(right)),
        out_specs=VMEM,
        scratch_shapes=[
            pltpu.VMEM((mu_rows, width), jnp.bfloat16),
            pltpu.VMEM((ratio * mu_rows, width), jnp.bfloat16),
        ],
    )(jnp.stack(places), *left, *right)


def solution(mesh):
    return jax.shard_map(
        body,
        mesh=mesh,
        in_specs=(
            P("row", "col", None, None, None, None),
            P("row", "col", None),
            P(("col", "row"), None),
            P("col", None),
        ),
        out_specs=P("row", "col"),
        check_vma=False,
    )
```

```python
import functools
import math

import jax
import jax.numpy as jnp
from jax import lax
from jax.experimental import pallas as pl
from jax.experimental.pallas import tpu as pltpu
from jax.sharding import PartitionSpec as P

VMEM = pl.BlockSpec(memory_space=pltpu.VMEM)
SMEM = pl.BlockSpec(memory_space=pltpu.SMEM)


class Layout:
    def __init__(self, n_row, n_col):
        self.n_row, self.n_col = n_row, n_col
        self.ratio = n_row // n_col
        self.groups = n_col // 4

    def permute(self, value, target):
        pairs = []
        for row in range(self.n_row):
            for col in range(self.n_col):
                plane, side, place = target(row // self.ratio, row % self.ratio, col)
                pairs.append((row * self.n_col + col, (plane * self.ratio + side) * self.n_col + place))
        return lax.ppermute(value, ("row", "col"), pairs)

    def shift(self, value, plane_bits=0, side_bits=0, col_bits=0):
        return self.permute(value, lambda z, y, w: (z ^ plane_bits, y ^ side_bits, w ^ col_bits))


def half_kernel(nu_blocks, block, place_ref, own_slots, next_slots, own_ref, next_ref, *refs):
    pieces, (out_ref, rows_ref) = refs[:-2], refs[-2:]
    rows, part = pieces[0].shape[1:]
    aux = own_ref.shape[1]
    for index, piece in enumerate(pieces):
        start = pl.multiple_of(place_ref[index] * rows, rows)
        rows_ref[:, pl.ds(start, rows), :] = piece[...]
    out_ref[...] = jnp.zeros_like(out_ref)

    def add(slot_ref, block_ref, side, slot):
        pair = slot_ref[slot]

        @pl.when(pair >= 0)
        def _():
            out_rows = pl.ds(pl.multiple_of(pair // nu_blocks * block, block), block)
            nu_rows = rows_ref[side, pl.ds(pl.multiple_of(pair % nu_blocks * block, block), block), :]
            for p in range(aux):
                columns = slice(p * part, (p + 1) * part)
                out_ref[out_rows, columns] += jnp.dot(
                    block_ref[slot, p], nu_rows, preferred_element_type=jnp.float32
                )

    @pl.loop(0, own_ref.shape[0])
    def _(slot):
        add(own_slots, own_ref, 0, slot)
        add(next_slots, next_ref, 1, slot)


def product_kernel(n_left, scale, place_ref, *refs):
    left, right, (out_ref, left_rows, right_rows) = refs[:n_left], refs[n_left:-3], refs[-3:]
    rows = left[0].shape[0]
    for index, piece in enumerate(left + right):
        target = left_rows if index < n_left else right_rows
        start = pl.multiple_of(place_ref[2 * index + 1], rows)
        target[place_ref[2 * index], pl.ds(start, rows), :] = piece[...]
    step = math.gcd(right_rows.shape[1], 256)
    for start in range(0, right_rows.shape[1], step):
        value = sum(
            lax.dot_general(
                left_rows[chip],
                right_rows[chip, start : start + step, :],
                (((1,), (1,)), ((), ())),
                preferred_element_type=jnp.float32,
            )
            for chip in range(2)
        )
        out_ref[:, start : start + step] = (value * scale).astype(out_ref.dtype)


def body(three_index, slot_pair, coeff, occ_mask):
    kept_slots, aux, block = three_index.shape[2:5]
    nu_rows, occ = coeff.shape
    n_row, n_col = lax.axis_size("row"), lax.axis_size("col")
    lay = Layout(n_row, n_col)
    ratio, groups = lay.ratio, lay.groups
    mu_rows, width, part = nu_rows * n_col, aux * occ, occ // 2
    nu_blocks = nu_rows * n_row // block
    row, col = lax.axis_index("row"), lax.axis_index("col")
    plane, side, group, chip = row // ratio, row % ratio, col // 4, col // 2 % 2

    blocks = three_index.reshape(kept_slots, aux, block, block)
    slots = slot_pair.reshape(kept_slots)
    kept = lax.dynamic_slice_in_dim(occ_mask, row * nu_rows // block, max(1, nu_rows // block), 0) != 0
    kept = jnp.repeat(jnp.repeat(kept, min(nu_rows, block), axis=0), block, axis=1)
    masked = jnp.where(kept, coeff, jnp.zeros_like(coeff))
    low, high = masked[:, :part], masked[:, part:]
    from_next = lay.shift(jnp.where(chip == 0, high, low), col_bits=2)
    shared = jnp.stack([jnp.where(chip == 0, low, high), from_next])
    next_slots = lay.shift(slots, col_bits=2)
    next_blocks = lay.shift(blocks, col_bits=2)

    pieces, places = [], []
    for d in range(n_col):
        here = lay.shift(shared, plane_bits=d) if d else shared
        for t in range(ratio):
            pieces.append(lay.shift(here, side_bits=t) if t else here)
            places.append((plane ^ d) * ratio + (side ^ t))
    partial = pl.pallas_call(
        functools.partial(half_kernel, nu_blocks, block),
        out_shape=jax.ShapeDtypeStruct((mu_rows, width // 2), jnp.float32),
        in_specs=[SMEM] * 3 + [VMEM] * (2 + len(pieces)),
        out_specs=VMEM,
        scratch_shapes=[pltpu.VMEM((2, nu_blocks * block, part), coeff.dtype)],
    )(jnp.stack(places), slots, next_slots, blocks, next_blocks, *pieces)

    total = partial + lay.shift(partial, col_bits=1)
    rows = mu_rows // groups
    if groups > 1:
        mine = [lax.dynamic_slice_in_dim(total, (group ^ e) * rows, rows, 0) for e in range(groups)]
        total = mine[0]
        for e in range(1, groups):
            total = total + lay.shift(mine[e], col_bits=4 * e)
    final = total.astype(jnp.bfloat16)

    left, right, places = [], [], []
    for e in range(2 * groups):
        left.append(lay.shift(final, col_bits=2 * e) if e else final)
        places += [(col // 2 ^ e) % 2, (col // 2 ^ e) // 2 * rows]
    for j in range(2 * groups):
        here = lay.permute(final, lambda z, y, w: (w % 2 * 2 * groups + (w // 2 ^ j), y, z))
        for t in range(ratio):
            right.append(lay.shift(here, side_bits=t) if t else here)
            source = plane % (2 * groups) ^ j
            places += [source % 2, (side ^ t) * mu_rows + source // 2 * rows]
    return pl.pallas_call(
        functools.partial(product_kernel, len(left), 1.0 / math.sqrt(width)),
        out_shape=jax.ShapeDtypeStruct((mu_rows, ratio * mu_rows), jnp.bfloat16),
        in_specs=[SMEM] + [VMEM] * (len(left) + len(right)),
        out_specs=VMEM,
        scratch_shapes=[
            pltpu.VMEM((2, mu_rows, width // 2), jnp.bfloat16),
            pltpu.VMEM((2, ratio * mu_rows, width // 2), jnp.bfloat16),
        ],
    )(jnp.stack(places), *left, *right)


def solution(mesh):
    return jax.shard_map(
        body,
        mesh=mesh,
        in_specs=(
            P("row", "col", None, None, None, None),
            P("row", "col", None),
            P(("col", "row"), None),
            P("col", None),
        ),
        out_specs=P("row", "col"),
        check_vma=False,
    )
```

```python
import functools
import math

import jax
import jax.numpy as jnp
from jax import lax
from jax.experimental import pallas as pl
from jax.experimental.pallas import tpu as pltpu
from jax.sharding import PartitionSpec as P


VMEM = pl.BlockSpec(memory_space=pltpu.VMEM)
SMEM = pl.BlockSpec(memory_space=pltpu.SMEM)
PARAMS = pltpu.CompilerParams(vmem_limit_bytes=16 << 20)


class Layout:
    def __init__(self, n_row, n_col):
        self.n_row, self.n_col = n_row, n_col
        self.ratio = n_row // n_col
        self.groups = n_col // 4

    def permute(self, value, target):
        pairs = []
        for row in range(self.n_row):
            for col in range(self.n_col):
                plane, side, place = target(row // self.ratio, row % self.ratio, col)
                pairs.append((row * self.n_col + col, (plane * self.ratio + side) * self.n_col + place))
        return lax.ppermute(value, ("row", "col"), pairs)

    def shift(self, value, plane_bits=0, side_bits=0, col_bits=0):
        return self.permute(value, lambda z, y, w: (z ^ plane_bits, y ^ side_bits, w ^ col_bits))


def share_kernel(own_ref, next_ref, out_ref):
    part = out_ref.shape[2]
    chip = lax.axis_index("col") >> 1 & 1
    columns = pl.ds(pl.multiple_of(chip * part, part), part)
    out_ref[0] = own_ref[:, columns]
    out_ref[1] = next_ref[:, columns]


def half_kernel(kept_slots, nu_blocks, block, place_ref, own_table, next_table, own_ref, next_ref, *refs):
    pieces, (out_ref, rows_ref, held_ref, sem) = refs[:-4], refs[-4:]
    rows, part = pieces[0].shape[1:]
    aux = own_ref.shape[1]
    copy = pltpu.make_async_copy(own_ref, held_ref, sem)
    copy.start()
    occ_blocks = 2 * part // block
    for index, piece in enumerate(pieces):
        start = pl.multiple_of(place_ref[1 + index] * rows, rows)
        for inner in range(0, rows, block):
            count = min(rows, block)
            mask_row = kept_slots + (start + inner) // block * occ_blocks + place_ref[0]
            for first in range(0, part, block):
                columns = slice(first, first + min(block, part))
                for side, table in enumerate((own_table, next_table)):
                    value = piece[side, inner : inner + count, columns]
                    kept = jnp.where(table[mask_row + first // block] != 0, value, jnp.zeros_like(value))
                    rows_ref[side, pl.ds(start + inner, count), columns] = kept
    out_ref[...] = jnp.zeros_like(out_ref)

    def add(table, block_ref, side, slot):
        pair = table[slot]

        @pl.when(pair >= 0)
        def _():
            out_rows = pl.ds(pl.multiple_of(pair // nu_blocks * block, block), block)
            nu_rows = rows_ref[side, pl.ds(pl.multiple_of(pair % nu_blocks * block, block), block), :]
            for p in range(aux):
                columns = slice(p * part, (p + 1) * part)
                out_ref[out_rows, columns] += jnp.dot(
                    block_ref[slot, p], nu_rows, preferred_element_type=jnp.float32
                )

    @pl.loop(0, kept_slots)
    def _(slot):
        add(next_table, next_ref, 1, slot)

    copy.wait()

    @pl.loop(0, kept_slots)
    def _(slot):
        add(own_table, held_ref, 0, slot)


def product_kernel(n_left, scale, place_ref, *refs):
    left, right, (out_ref, left_rows, right_rows) = refs[:n_left], refs[n_left:-3], refs[-3:]
    rows = left[0].shape[0]
    for index, piece in enumerate(left + right):
        target = left_rows if index < n_left else right_rows
        start = pl.multiple_of(place_ref[2 * index + 1], rows)
        target[place_ref[2 * index], pl.ds(start, rows), :] = piece[...]
    step = math.gcd(right_rows.shape[1], 256)
    for start in range(0, right_rows.shape[1], step):
        value = sum(
            lax.dot_general(
                left_rows[chip],
                right_rows[chip, start : start + step, :],
                (((1,), (1,)), ((), ())),
                preferred_element_type=jnp.float32,
            )
            for chip in range(2)
        )
        out_ref[:, start : start + step] = (value * scale).astype(out_ref.dtype)


def exchange(three_index, slot_pair, coeff, occ_mask):
    kept_slots, aux, block = three_index.shape[2:5]
    nu_rows, occ = coeff.shape
    n_row, n_col = lax.axis_size("row"), lax.axis_size("col")
    lay = Layout(n_row, n_col)
    ratio, groups = lay.ratio, lay.groups
    mu_rows, width, part = nu_rows * n_col, aux * occ, occ // 2
    nu_blocks = nu_rows * n_row // block
    row, col = lax.axis_index("row"), lax.axis_index("col")
    plane, side, group, chip = row // ratio, row % ratio, col // 4, col // 2 % 2

    blocks = three_index.reshape(kept_slots, aux, block, block)
    table = jnp.concatenate([slot_pair.reshape(kept_slots), occ_mask.reshape(-1)])
    next_coeff = lay.shift(coeff, col_bits=2)
    next_table = lay.shift(table, col_bits=2)
    next_blocks = lay.shift(blocks, col_bits=2)
    shared = pl.pallas_call(
        share_kernel,
        out_shape=jax.ShapeDtypeStruct((2, nu_rows, part), coeff.dtype),
        in_specs=[VMEM, VMEM],
        out_specs=VMEM,
        compiler_params=PARAMS,
    )(coeff, next_coeff)

    pieces, places = [], []
    for d in range(n_col):
        here = lay.shift(shared, plane_bits=d) if d else shared
        for t in range(ratio):
            pieces.append(lay.shift(here, side_bits=t) if t else here)
            places.append((plane ^ d) * ratio + (side ^ t))
    partial = pl.pallas_call(
        functools.partial(half_kernel, kept_slots, nu_blocks, block),
        out_shape=jax.ShapeDtypeStruct((mu_rows, width // 2), jnp.float32),
        in_specs=[SMEM] * 3 + [pl.BlockSpec(memory_space=pl.ANY)] + [VMEM] * (1 + len(pieces)),
        out_specs=VMEM,
        scratch_shapes=[
            pltpu.VMEM((2, nu_blocks * block, part), coeff.dtype),
            pltpu.VMEM(blocks.shape, blocks.dtype),
            pltpu.SemaphoreType.DMA,
        ],
        compiler_params=PARAMS,
    )(jnp.stack([chip * part // block] + places), table, next_table, blocks, next_blocks, *pieces)

    total = partial + lay.shift(partial, col_bits=1)
    rows = mu_rows // groups
    if groups > 1:
        mine = [lax.dynamic_slice_in_dim(total, (group ^ e) * rows, rows, 0) for e in range(groups)]
        total = mine[0]
        for e in range(1, groups):
            total = total + lay.shift(mine[e], col_bits=4 * e)
    final = total.astype(jnp.bfloat16)

    left, right, places = [], [], []
    for e in range(2 * groups):
        left.append(lay.shift(final, col_bits=2 * e) if e else final)
        places += [(col // 2 ^ e) % 2, (col // 2 ^ e) // 2 * rows]
    for j in range(2 * groups):
        here = lay.permute(final, lambda z, y, w: (w % 2 * 2 * groups + (w // 2 ^ j), y, z))
        for t in range(ratio):
            right.append(lay.shift(here, side_bits=t) if t else here)
            source = plane % (2 * groups) ^ j
            places += [source % 2, (side ^ t) * mu_rows + source // 2 * rows]
    return pl.pallas_call(
        functools.partial(product_kernel, len(left), 1.0 / math.sqrt(width)),
        out_shape=jax.ShapeDtypeStruct((mu_rows, ratio * mu_rows), jnp.bfloat16),
        in_specs=[SMEM] + [VMEM] * (len(left) + len(right)),
        out_specs=VMEM,
        scratch_shapes=[
            pltpu.VMEM((2, mu_rows, width // 2), jnp.bfloat16),
            pltpu.VMEM((2, ratio * mu_rows, width // 2), jnp.bfloat16),
        ],
        compiler_params=PARAMS,
    )(jnp.stack(places), *left, *right)


def solution(mesh):
    return jax.shard_map(
        exchange,
        mesh=mesh,
        in_specs=(
            P("row", "col", None, None, None, None),
            P("row", "col", None),
            P(("col", "row"), None),
            P("col", None),
        ),
        out_specs=P("row", "col"),
        check_vma=False,
    )
```

```python
import functools
import math

import jax
import jax.numpy as jnp
from jax import lax
from jax.experimental import pallas as pl
from jax.experimental.pallas import tpu as pltpu
from jax.sharding import PartitionSpec as P


VMEM = pl.BlockSpec(memory_space=pltpu.VMEM)
SMEM = pl.BlockSpec(memory_space=pltpu.SMEM)
PARAMS = pltpu.CompilerParams(vmem_limit_bytes=16 << 20)


class Layout:
    def __init__(self, n_row, n_col):
        self.n_row, self.n_col = n_row, n_col
        self.ratio = n_row // n_col
        self.groups = n_col // 4

    def permute(self, value, target):
        pairs = []
        for row in range(self.n_row):
            for col in range(self.n_col):
                plane, side, place = target(row // self.ratio, row % self.ratio, col)
                pairs.append((row * self.n_col + col, (plane * self.ratio + side) * self.n_col + place))
        return lax.ppermute(value, ("row", "col"), pairs)

    def shift(self, value, plane_bits=0, side_bits=0, col_bits=0):
        return self.permute(value, lambda z, y, w: (z ^ plane_bits, y ^ side_bits, w ^ col_bits))


def chip_half(ref, part):
    chip = lax.axis_index("col") >> 1 & 1
    return ref[:, pl.ds(pl.multiple_of(chip * part, part), part)]


def own_kernel(own_ref, out_ref):
    out_ref[0] = chip_half(own_ref, out_ref.shape[2])


def next_kernel(next_ref, held_ref, out_ref):
    out_ref[1] = chip_half(next_ref, out_ref.shape[2])


def half_kernel(kept_slots, nu_blocks, block, place_ref, own_table, next_table, own_ref, next_ref, *refs):
    pieces, (out_ref, rows_ref, held_ref, sem) = refs[:-4], refs[-4:]
    rows, part = pieces[0].shape[1:]
    aux = own_ref.shape[1]
    copy = pltpu.make_async_copy(own_ref, held_ref, sem)
    copy.start()
    occ_blocks = 2 * part // block
    for index, piece in enumerate(pieces):
        start = pl.multiple_of(place_ref[1 + index] * rows, rows)
        for inner in range(0, rows, block):
            count = min(rows, block)
            mask_row = kept_slots + (start + inner) // block * occ_blocks + place_ref[0]
            for first in range(0, part, block):
                columns = slice(first, first + min(block, part))
                for side, table in enumerate((own_table, next_table)):
                    value = piece[side, inner : inner + count, columns]
                    kept = jnp.where(table[mask_row + first // block] != 0, value, jnp.zeros_like(value))
                    rows_ref[side, pl.ds(start + inner, count), columns] = kept
    out_ref[...] = jnp.zeros_like(out_ref)

    def add(table, block_ref, side, slot):
        pair = table[slot]

        @pl.when(pair >= 0)
        def _():
            out_rows = pl.ds(pl.multiple_of(pair // nu_blocks * block, block), block)
            nu_rows = rows_ref[side, pl.ds(pl.multiple_of(pair % nu_blocks * block, block), block), :]
            for p in range(aux):
                columns = slice(p * part, (p + 1) * part)
                out_ref[out_rows, columns] += jnp.dot(
                    block_ref[slot, p], nu_rows, preferred_element_type=jnp.float32
                )

    @pl.loop(0, kept_slots)
    def _(slot):
        add(next_table, next_ref, 1, slot)

    copy.wait()

    @pl.loop(0, kept_slots)
    def _(slot):
        add(own_table, held_ref, 0, slot)


def product_kernel(n_left, scale, place_ref, *refs):
    left, right = refs[:n_left], refs[n_left : 2 * n_left]
    out_ref, left_rows, right_rows, tiles, sems = refs[-5:]
    rows = left[0].shape[0]
    for index in range(n_left):
        for base, pieces, held in ((1, left, left_rows), (1 + 2 * n_left, right, right_rows)):
            start = pl.multiple_of(place_ref[base + 2 * index + 1], rows)
            held[place_ref[base + 2 * index], pl.ds(start, rows), :] = pieces[index][...]
    width = tiles.shape[2]
    copies = []
    for tile in range(tiles.shape[0]):
        value = sum(
            lax.dot_general(
                left_rows[chip],
                right_rows[chip, tile * width : (tile + 1) * width, :],
                (((1,), (1,)), ((), ())),
                preferred_element_type=jnp.float32,
            )
            for chip in range(2)
        )
        tiles[tile] = (value * scale).astype(tiles.dtype)
        first = pl.multiple_of(place_ref[0] + tile * width, width)
        copies.append(pltpu.make_async_copy(tiles.at[tile], out_ref.at[:, pl.ds(first, width)], sems.at[tile]))
        copies[-1].start()
    for copy in copies:
        copy.wait()


def exchange(three_index, slot_pair, coeff, occ_mask):
    kept_slots, aux, block = three_index.shape[2:5]
    nu_rows, occ = coeff.shape
    n_row, n_col = lax.axis_size("row"), lax.axis_size("col")
    lay = Layout(n_row, n_col)
    ratio, groups = lay.ratio, lay.groups
    mu_rows, width, part = nu_rows * n_col, aux * occ, occ // 2
    nu_blocks = nu_rows * n_row // block
    row, col = lax.axis_index("row"), lax.axis_index("col")
    plane, side, group, chip = row // ratio, row % ratio, col // 4, col // 2 % 2

    blocks = three_index.reshape(kept_slots, aux, block, block)
    table = jnp.concatenate([slot_pair.reshape(kept_slots), occ_mask.reshape(-1)])
    next_coeff = lay.shift(coeff, col_bits=2)
    next_table = lay.shift(table, col_bits=2)
    next_blocks = lay.shift(blocks, col_bits=2)
    shared = pl.pallas_call(
        own_kernel,
        out_shape=jax.ShapeDtypeStruct((2, nu_rows, part), coeff.dtype),
        in_specs=[VMEM],
        out_specs=VMEM,
        compiler_params=PARAMS,
    )(coeff)
    shared = pl.pallas_call(
        next_kernel,
        out_shape=jax.ShapeDtypeStruct((2, nu_rows, part), coeff.dtype),
        in_specs=[VMEM, VMEM],
        out_specs=VMEM,
        input_output_aliases={1: 0},
        compiler_params=PARAMS,
    )(next_coeff, shared)

    pieces, places = [], []
    for d in range(n_col):
        here = lay.shift(shared, plane_bits=d) if d else shared
        for t in range(ratio):
            pieces.append(lay.shift(here, side_bits=t) if t else here)
            places.append((plane ^ d) * ratio + (side ^ t))
    partial = pl.pallas_call(
        functools.partial(half_kernel, kept_slots, nu_blocks, block),
        out_shape=jax.ShapeDtypeStruct((mu_rows, width // 2), jnp.float32),
        in_specs=[SMEM] * 3 + [pl.BlockSpec(memory_space=pltpu.HBM)] + [VMEM] * (1 + len(pieces)),
        out_specs=VMEM,
        scratch_shapes=[
            pltpu.VMEM((2, nu_blocks * block, part), coeff.dtype),
            pltpu.VMEM(blocks.shape, blocks.dtype),
            pltpu.SemaphoreType.DMA,
        ],
        compiler_params=PARAMS,
    )(jnp.stack([chip * part // block] + places), table, next_table, blocks, next_blocks, *pieces)

    total = partial + lay.shift(partial, col_bits=1)
    rows = mu_rows // groups
    if groups > 1:
        mine = [lax.dynamic_slice_in_dim(total, (group ^ e) * rows, rows, 0) for e in range(groups)]
        total = mine[0]
        for e in range(1, groups):
            total = total + lay.shift(mine[e], col_bits=4 * e)
    final = total.astype(jnp.bfloat16)

    pieces = 2 * groups
    left, left_places = [], []
    for e in range(pieces):
        left.append(lay.shift(final, col_bits=2 * e) if e else final)
        left_places += [(col // 2 ^ e) % 2, (col // 2 ^ e) // 2 * rows]
    sources = [lay.permute(final, lambda z, y, w: (w % 2 * pieces + (w // 2 ^ j), y, z)) for j in range(pieces)]
    source_places = []
    for j in range(pieces):
        source_places += [(plane % pieces ^ j) % 2, (plane % pieces ^ j) // 2 * rows]

    out = ()
    columns = math.gcd(mu_rows, 256)
    for t in range(ratio):
        right = [lay.shift(piece, side_bits=t) if t else piece for piece in sources]
        out = pl.pallas_call(
            functools.partial(product_kernel, pieces, 1.0 / math.sqrt(width)),
            out_shape=(jax.ShapeDtypeStruct((mu_rows, ratio * mu_rows), jnp.bfloat16),),
            in_specs=[SMEM] + [VMEM] * (2 * pieces) + [pl.BlockSpec(memory_space=pltpu.HBM)] * len(out),
            out_specs=(pl.BlockSpec(memory_space=pltpu.HBM),),
            input_output_aliases={1 + 2 * pieces: 0} if out else {},
            scratch_shapes=[
                pltpu.VMEM((2, mu_rows, width // 2), jnp.bfloat16),
                pltpu.VMEM((2, mu_rows, width // 2), jnp.bfloat16),
                pltpu.VMEM((mu_rows // columns, mu_rows, columns), jnp.bfloat16),
                pltpu.SemaphoreType.DMA((mu_rows // columns,)),
            ],
            compiler_params=PARAMS,
        )(jnp.stack([(side ^ t) * mu_rows] + left_places + source_places), *left, *right, *out)
    return out[0]


def solution(mesh):
    return jax.shard_map(
        exchange,
        mesh=mesh,
        in_specs=(
            P("row", "col", None, None, None, None),
            P("row", "col", None),
            P(("col", "row"), None),
            P("col", None),
        ),
        out_specs=P("row", "col"),
        check_vma=False,
    )
```

```python
import functools
import math

import jax
import jax.numpy as jnp
from jax import lax
from jax.experimental import pallas as pl
from jax.experimental.pallas import tpu as pltpu
from jax.sharding import PartitionSpec as P


VMEM = pl.BlockSpec(memory_space=pltpu.VMEM)
HBM = pl.BlockSpec(memory_space=pltpu.HBM)
SMEM = pl.BlockSpec(memory_space=pltpu.SMEM)
PARAMS = pltpu.CompilerParams(vmem_limit_bytes=16 << 20)


class Layout:
    def __init__(self, n_row, n_col):
        self.n_row, self.n_col = n_row, n_col
        self.ratio = n_row // n_col
        self.groups = n_col // 4

    def permute(self, value, target):
        pairs = []
        for row in range(self.n_row):
            for col in range(self.n_col):
                plane, side, place = target(row // self.ratio, row % self.ratio, col)
                pairs.append((row * self.n_col + col, (plane * self.ratio + side) * self.n_col + place))
        return lax.ppermute(value, ("row", "col"), pairs)

    def shift(self, value, plane_bits=0, side_bits=0, col_bits=0):
        return self.permute(value, lambda z, y, w: (z ^ plane_bits, y ^ side_bits, w ^ col_bits))


def chip_half(ref, part):
    chip = lax.axis_index("col") >> 1 & 1
    return ref[:, pl.ds(pl.multiple_of(chip * part, part), part)]


def own_kernel(coeff_ref, blocks_ref, out_ref, held_ref, coeff_held, sems):
    copies = [
        pltpu.make_async_copy(coeff_ref, coeff_held, sems.at[0]),
        pltpu.make_async_copy(blocks_ref, held_ref, sems.at[1]),
    ]
    for copy in copies:
        copy.start()
    copies[0].wait()
    out_ref[0] = chip_half(coeff_held, out_ref.shape[2])
    copies[1].wait()


def next_kernel(next_ref, held_ref, out_ref):
    out_ref[1] = chip_half(next_ref, out_ref.shape[2])


def half_kernel(
    kept_slots, nu_blocks, block, place_ref, own_slots, next_slots, own_mask, next_mask, own_ref, next_ref, *refs
):
    pieces, (out_ref, rows_ref) = refs[:-2], refs[-2:]
    rows, part = pieces[0].shape[1:]
    aux = own_ref.shape[1]
    for index, piece in enumerate(pieces):
        start = pl.multiple_of(place_ref[1 + index] * rows, rows)
        for inner in range(0, rows, block):
            count = min(rows, block)
            nu_block = (start + inner) // block
            for first in range(0, part, block):
                columns = slice(first, first + min(block, part))
                for side, mask in enumerate((own_mask, next_mask)):
                    value = piece[side, inner : inner + count, columns]
                    kept = jnp.where(mask[place_ref[0] + first // block, nu_block] != 0, value, jnp.zeros_like(value))
                    rows_ref[side, pl.ds(start + inner, count), columns] = kept
    out_ref[...] = jnp.zeros_like(out_ref)

    def add(slots, block_ref, side, slot):
        pair = slots[slot]

        @pl.when(pair >= 0)
        def _():
            out_rows = pl.ds(pl.multiple_of(pair // nu_blocks * block, block), block)
            nu_rows = rows_ref[side, pl.ds(pl.multiple_of(pair % nu_blocks * block, block), block), :]
            for p in range(aux):
                columns = slice(p * part, (p + 1) * part)
                out_ref[out_rows, columns] += jnp.dot(
                    block_ref[slot, p], nu_rows, preferred_element_type=jnp.float32
                )

    @pl.loop(0, kept_slots)
    def _(slot):
        add(own_slots, own_ref, 0, slot)
        add(next_slots, next_ref, 1, slot)


def product_kernel(n_left, scale, place_ref, *refs):
    left, right = refs[:n_left], refs[n_left : 2 * n_left]
    out_ref, left_rows, right_rows, tiles, sems = refs[-5:]
    rows = left[0].shape[0]
    for index in range(n_left):
        for base, pieces, held in ((1, left, left_rows), (1 + 2 * n_left, right, right_rows)):
            start = pl.multiple_of(place_ref[base + 2 * index + 1], rows)
            held[place_ref[base + 2 * index], pl.ds(start, rows), :] = pieces[index][...]
    width = tiles.shape[2]
    copies = []
    for tile in range(tiles.shape[0]):
        value = sum(
            lax.dot_general(
                left_rows[chip],
                right_rows[chip, tile * width : (tile + 1) * width, :],
                (((1,), (1,)), ((), ())),
                preferred_element_type=jnp.float32,
            )
            for chip in range(2)
        )
        tiles[tile] = (value * scale).astype(tiles.dtype)
        first = pl.multiple_of(place_ref[0] + tile * width, width)
        copies.append(pltpu.make_async_copy(tiles.at[tile], out_ref.at[:, pl.ds(first, width)], sems.at[tile]))
        copies[-1].start()
    for copy in copies:
        copy.wait()


def exchange(three_index, slot_pair, coeff, occ_mask):
    kept_slots, aux, block = three_index.shape[2:5]
    nu_rows, occ = coeff.shape
    n_row, n_col = lax.axis_size("row"), lax.axis_size("col")
    lay = Layout(n_row, n_col)
    ratio, groups = lay.ratio, lay.groups
    mu_rows, width, part = nu_rows * n_col, aux * occ, occ // 2
    nu_blocks = nu_rows * n_row // block
    row, col = lax.axis_index("row"), lax.axis_index("col")
    plane, side, group, chip = row // ratio, row % ratio, col // 4, col // 2 % 2

    blocks = three_index.reshape(kept_slots, aux, block, block)
    slots, mask = slot_pair.reshape(kept_slots), occ_mask.T
    next_coeff = lay.shift(coeff, col_bits=2)
    next_slots = lay.shift(slots, col_bits=2)
    next_mask = lay.shift(mask, col_bits=2)
    next_blocks = lay.shift(blocks, col_bits=2)
    shared, blocks = pl.pallas_call(
        own_kernel,
        out_shape=(
            jax.ShapeDtypeStruct((2, nu_rows, part), coeff.dtype),
            jax.ShapeDtypeStruct(blocks.shape, blocks.dtype),
        ),
        in_specs=[HBM, HBM],
        out_specs=(VMEM, VMEM),
        scratch_shapes=[pltpu.VMEM(coeff.shape, coeff.dtype), pltpu.SemaphoreType.DMA((2,))],
        compiler_params=PARAMS,
    )(coeff, blocks)
    shared = pl.pallas_call(
        next_kernel,
        out_shape=jax.ShapeDtypeStruct((2, nu_rows, part), coeff.dtype),
        in_specs=[VMEM, VMEM],
        out_specs=VMEM,
        input_output_aliases={1: 0},
        compiler_params=PARAMS,
    )(next_coeff, shared)

    pieces, places = [], []
    for d in range(n_col):
        here = lay.shift(shared, plane_bits=d) if d else shared
        for t in range(ratio):
            pieces.append(lay.shift(here, side_bits=t) if t else here)
            places.append((plane ^ d) * ratio + (side ^ t))
    partial = pl.pallas_call(
        functools.partial(half_kernel, kept_slots, nu_blocks, block),
        out_shape=jax.ShapeDtypeStruct((mu_rows, width // 2), jnp.float32),
        in_specs=[SMEM] * 5 + [VMEM] * (2 + len(pieces)),
        out_specs=VMEM,
        scratch_shapes=[pltpu.VMEM((2, nu_blocks * block, part), coeff.dtype)],
        compiler_params=PARAMS,
    )(jnp.stack([chip * part // block] + places), slots, next_slots, mask, next_mask, blocks, next_blocks, *pieces)

    total = partial + lay.shift(partial, col_bits=1)
    rows = mu_rows // groups
    if groups > 1:
        mine = [lax.dynamic_slice_in_dim(total, (group ^ e) * rows, rows, 0) for e in range(groups)]
        total = mine[0]
        for e in range(1, groups):
            total = total + lay.shift(mine[e], col_bits=4 * e)
    final = total.astype(jnp.bfloat16)

    pieces = 2 * groups
    left, left_places = [], []
    for e in range(pieces):
        left.append(lay.shift(final, col_bits=2 * e) if e else final)
        left_places += [(col // 2 ^ e) % 2, (col // 2 ^ e) // 2 * rows]
    sources = [lay.permute(final, lambda z, y, w: (w % 2 * pieces + (w // 2 ^ j), y, z)) for j in range(pieces)]
    source_places = []
    for j in range(pieces):
        source_places += [(plane % pieces ^ j) % 2, (plane % pieces ^ j) // 2 * rows]

    out = ()
    columns = math.gcd(mu_rows, 256)
    for t in range(ratio):
        right = [lay.shift(piece, side_bits=t) if t else piece for piece in sources]
        out = pl.pallas_call(
            functools.partial(product_kernel, pieces, 1.0 / math.sqrt(width)),
            out_shape=(jax.ShapeDtypeStruct((mu_rows, ratio * mu_rows), jnp.bfloat16),),
            in_specs=[SMEM] + [VMEM] * (2 * pieces) + [HBM] * len(out),
            out_specs=(HBM,),
            input_output_aliases={1 + 2 * pieces: 0} if out else {},
            scratch_shapes=[
                pltpu.VMEM((2, mu_rows, width // 2), jnp.bfloat16),
                pltpu.VMEM((2, mu_rows, width // 2), jnp.bfloat16),
                pltpu.VMEM((mu_rows // columns, mu_rows, columns), jnp.bfloat16),
                pltpu.SemaphoreType.DMA((mu_rows // columns,)),
            ],
            compiler_params=PARAMS,
        )(jnp.stack([(side ^ t) * mu_rows] + left_places + source_places), *left, *right, *out)
    return out[0]


def solution(mesh):
    return jax.shard_map(
        exchange,
        mesh=mesh,
        in_specs=(
            P("row", "col", None, None, None, None),
            P("row", "col", None),
            P(("col", "row"), None),
            P("col", None),
        ),
        out_specs=P("row", "col"),
        check_vma=False,
    )
```

```python
import functools
import math

import jax
import jax.numpy as jnp
from jax import lax
from jax.experimental import pallas as pl
from jax.experimental.pallas import tpu as pltpu
from jax.sharding import PartitionSpec as P


VMEM = pl.BlockSpec(memory_space=pltpu.VMEM)
HBM = pl.BlockSpec(memory_space=pltpu.HBM)
TABLE = (8, 128)
SMEM = pl.BlockSpec(memory_space=pltpu.SMEM)
PARAMS = pltpu.CompilerParams(vmem_limit_bytes=16 << 20)


class Layout:
    def __init__(self, n_row, n_col):
        self.n_row, self.n_col = n_row, n_col
        self.ratio = n_row // n_col
        self.groups = n_col // 4

    def permute(self, value, target):
        pairs = []
        for row in range(self.n_row):
            for col in range(self.n_col):
                plane, side, place = target(row // self.ratio, row % self.ratio, col)
                pairs.append((row * self.n_col + col, (plane * self.ratio + side) * self.n_col + place))
        return lax.ppermute(value, ("row", "col"), pairs)

    def shift(self, value, plane_bits=0, side_bits=0, col_bits=0):
        return self.permute(value, lambda z, y, w: (z ^ plane_bits, y ^ side_bits, w ^ col_bits))


def chip_half(ref, part):
    chip = lax.axis_index("col") >> 1 & 1
    return ref[:, pl.ds(pl.multiple_of(chip * part, part), part)]


def own_kernel(slot_ref, mask_ref, coeff_ref, blocks_ref, out_ref, held_ref, table_ref, coeff_held, sems):
    copies = [
        pltpu.make_async_copy(coeff_ref, coeff_held, sems.at[0]),
        pltpu.make_async_copy(blocks_ref, held_ref, sems.at[1]),
    ]
    for copy in copies:
        copy.start()
    line = lax.broadcasted_iota(jnp.int32, TABLE, 0)
    lane = lax.broadcasted_iota(jnp.int32, TABLE, 1)
    table = jnp.zeros(TABLE, jnp.int32)
    for slot in range(slot_ref.shape[0]):
        table = jnp.where((line == 0) & (lane == slot), slot_ref[slot], table)
    for part in range(mask_ref.shape[0]):
        for nu_block in range(mask_ref.shape[1]):
            table = jnp.where((line == 1 + part) & (lane == nu_block), mask_ref[part, nu_block], table)
    table_ref[...] = table
    copies[0].wait()
    out_ref[0] = chip_half(coeff_held, out_ref.shape[2])
    copies[1].wait()


def next_kernel(next_ref, held_ref, out_ref):
    out_ref[1] = chip_half(next_ref, out_ref.shape[2])


def half_kernel(
    kept_slots, nu_blocks, block, place_ref, own_table, next_table, own_ref, next_ref, *refs
):
    pieces, (out_ref, rows_ref) = refs[:-2], refs[-2:]
    rows, part = pieces[0].shape[1:]
    aux = own_ref.shape[1]
    for index, piece in enumerate(pieces):
        start = pl.multiple_of(place_ref[1 + index] * rows, rows)
        for inner in range(0, rows, block):
            count = min(rows, block)
            nu_block = (start + inner) // block
            for first in range(0, part, block):
                columns = slice(first, first + min(block, part))
                for side, table in enumerate((own_table, next_table)):
                    value = piece[side, inner : inner + count, columns]
                    kept = jnp.where(table[1 + place_ref[0] + first // block, nu_block] != 0, value, jnp.zeros_like(value))
                    rows_ref[side, pl.ds(start + inner, count), columns] = kept
    out_ref[...] = jnp.zeros_like(out_ref)

    def add(table, block_ref, side, slot):
        pair = table[0, slot]

        @pl.when(pair >= 0)
        def _():
            out_rows = pl.ds(pl.multiple_of(pair // nu_blocks * block, block), block)
            nu_rows = rows_ref[side, pl.ds(pl.multiple_of(pair % nu_blocks * block, block), block), :]
            for p in range(aux):
                columns = slice(p * part, (p + 1) * part)
                out_ref[out_rows, columns] += jnp.dot(
                    block_ref[slot, p], nu_rows, preferred_element_type=jnp.float32
                )

    @pl.loop(0, kept_slots)
    def _(slot):
        add(own_table, own_ref, 0, slot)
        add(next_table, next_ref, 1, slot)


def product_kernel(n_left, scale, place_ref, *refs):
    left, right = refs[:n_left], refs[n_left : 2 * n_left]
    out_ref, left_rows, right_rows, tiles, sems = refs[-5:]
    rows = left[0].shape[0]
    for index in range(n_left):
        for base, pieces, held in ((1, left, left_rows), (1 + 2 * n_left, right, right_rows)):
            start = pl.multiple_of(place_ref[base + 2 * index + 1], rows)
            held[place_ref[base + 2 * index], pl.ds(start, rows), :] = pieces[index][...]
    width = tiles.shape[2]
    copies = []
    for tile in range(tiles.shape[0]):
        value = sum(
            lax.dot_general(
                left_rows[chip],
                right_rows[chip, tile * width : (tile + 1) * width, :],
                (((1,), (1,)), ((), ())),
                preferred_element_type=jnp.float32,
            )
            for chip in range(2)
        )
        tiles[tile] = (value * scale).astype(tiles.dtype)
        first = pl.multiple_of(place_ref[0] + tile * width, width)
        copies.append(pltpu.make_async_copy(tiles.at[tile], out_ref.at[:, pl.ds(first, width)], sems.at[tile]))
        copies[-1].start()
    for copy in copies:
        copy.wait()


def exchange(three_index, slot_pair, coeff, occ_mask):
    kept_slots, aux, block = three_index.shape[2:5]
    nu_rows, occ = coeff.shape
    n_row, n_col = lax.axis_size("row"), lax.axis_size("col")
    lay = Layout(n_row, n_col)
    ratio, groups = lay.ratio, lay.groups
    mu_rows, width, part = nu_rows * n_col, aux * occ, occ // 2
    nu_blocks = nu_rows * n_row // block
    row, col = lax.axis_index("row"), lax.axis_index("col")
    plane, side, group, chip = row // ratio, row % ratio, col // 4, col // 2 % 2

    blocks = three_index.reshape(kept_slots, aux, block, block)
    slots, mask = slot_pair.reshape(kept_slots), occ_mask.T
    next_coeff = lay.shift(coeff, col_bits=2)
    shared, blocks, table = pl.pallas_call(
        own_kernel,
        out_shape=(
            jax.ShapeDtypeStruct((2, nu_rows, part), coeff.dtype),
            jax.ShapeDtypeStruct(blocks.shape, blocks.dtype),
            jax.ShapeDtypeStruct(TABLE, jnp.int32),
        ),
        in_specs=[SMEM, SMEM, HBM, HBM],
        out_specs=(VMEM, VMEM, VMEM),
        scratch_shapes=[pltpu.VMEM(coeff.shape, coeff.dtype), pltpu.SemaphoreType.DMA((2,))],
        compiler_params=PARAMS,
    )(slots, mask, coeff, blocks)
    next_table = lay.shift(table, col_bits=2)
    next_blocks = lay.shift(blocks, col_bits=2)
    shared = pl.pallas_call(
        next_kernel,
        out_shape=jax.ShapeDtypeStruct((2, nu_rows, part), coeff.dtype),
        in_specs=[VMEM, VMEM],
        out_specs=VMEM,
        input_output_aliases={1: 0},
        compiler_params=PARAMS,
    )(next_coeff, shared)

    pieces, places = [], []
    for d in range(n_col):
        here = lay.shift(shared, plane_bits=d) if d else shared
        for t in range(ratio):
            pieces.append(lay.shift(here, side_bits=t) if t else here)
            places.append((plane ^ d) * ratio + (side ^ t))
    partial = pl.pallas_call(
        functools.partial(half_kernel, kept_slots, nu_blocks, block),
        out_shape=jax.ShapeDtypeStruct((mu_rows, width // 2), jnp.float32),
        in_specs=[SMEM] * 3 + [VMEM] * (2 + len(pieces)),
        out_specs=VMEM,
        scratch_shapes=[pltpu.VMEM((2, nu_blocks * block, part), coeff.dtype)],
        compiler_params=PARAMS,
    )(jnp.stack([chip * part // block] + places), table, next_table, blocks, next_blocks, *pieces)

    total = partial + lay.shift(partial, col_bits=1)
    rows = mu_rows // groups
    if groups > 1:
        mine = [lax.dynamic_slice_in_dim(total, (group ^ e) * rows, rows, 0) for e in range(groups)]
        total = mine[0]
        for e in range(1, groups):
            total = total + lay.shift(mine[e], col_bits=4 * e)
    final = total.astype(jnp.bfloat16)

    pieces = 2 * groups
    left, left_places = [], []
    for e in range(pieces):
        left.append(lay.shift(final, col_bits=2 * e) if e else final)
        left_places += [(col // 2 ^ e) % 2, (col // 2 ^ e) // 2 * rows]
    sources = [lay.permute(final, lambda z, y, w: (w % 2 * pieces + (w // 2 ^ j), y, z)) for j in range(pieces)]
    source_places = []
    for j in range(pieces):
        source_places += [(plane % pieces ^ j) % 2, (plane % pieces ^ j) // 2 * rows]

    out = ()
    columns = math.gcd(mu_rows, 256)
    for t in range(ratio):
        right = [lay.shift(piece, side_bits=t) if t else piece for piece in sources]
        out = pl.pallas_call(
            functools.partial(product_kernel, pieces, 1.0 / math.sqrt(width)),
            out_shape=(jax.ShapeDtypeStruct((mu_rows, ratio * mu_rows), jnp.bfloat16),),
            in_specs=[SMEM] + [VMEM] * (2 * pieces) + [HBM] * len(out),
            out_specs=(HBM,),
            input_output_aliases={1 + 2 * pieces: 0} if out else {},
            scratch_shapes=[
                pltpu.VMEM((2, mu_rows, width // 2), jnp.bfloat16),
                pltpu.VMEM((2, mu_rows, width // 2), jnp.bfloat16),
                pltpu.VMEM((mu_rows // columns, mu_rows, columns), jnp.bfloat16),
                pltpu.SemaphoreType.DMA((mu_rows // columns,)),
            ],
            compiler_params=PARAMS,
        )(jnp.stack([(side ^ t) * mu_rows] + left_places + source_places), *left, *right, *out)
    return out[0]


def solution(mesh):
    return jax.shard_map(
        exchange,
        mesh=mesh,
        in_specs=(
            P("row", "col", None, None, None, None),
            P("row", "col", None),
            P(("col", "row"), None),
            P("col", None),
        ),
        out_specs=P("row", "col"),
        check_vma=False,
    )
```

```python
import functools
import math

import jax
import jax.numpy as jnp
from jax import lax
from jax.experimental import pallas as pl
from jax.experimental.pallas import tpu as pltpu
from jax.sharding import PartitionSpec as P


VMEM = pl.BlockSpec(memory_space=pltpu.VMEM)
HBM = pl.BlockSpec(memory_space=pltpu.HBM)
TABLE = (8, 128)
SMEM = pl.BlockSpec(memory_space=pltpu.SMEM)
PARAMS = pltpu.CompilerParams(vmem_limit_bytes=16 << 20)


class Layout:
    def __init__(self, n_row, n_col):
        self.n_row, self.n_col = n_row, n_col
        self.ratio = n_row // n_col
        self.groups = n_col // 4

    def permute(self, value, target):
        pairs = []
        for row in range(self.n_row):
            for col in range(self.n_col):
                plane, side, place = target(row // self.ratio, row % self.ratio, col)
                pairs.append((row * self.n_col + col, (plane * self.ratio + side) * self.n_col + place))
        return lax.ppermute(value, ("row", "col"), pairs)

    def shift(self, value, plane_bits=0, side_bits=0, col_bits=0):
        return self.permute(value, lambda z, y, w: (z ^ plane_bits, y ^ side_bits, w ^ col_bits))


def chip_half(ref, part):
    chip = lax.axis_index("col") >> 1 & 1
    return ref[:, pl.ds(pl.multiple_of(chip * part, part), part)]


def own_kernel(slot_ref, mask_ref, coeff_ref, blocks_ref, out_ref, held_ref, table_ref, coeff_held, sems):
    copies = [
        pltpu.make_async_copy(coeff_ref, coeff_held, sems.at[0]),
        pltpu.make_async_copy(blocks_ref, held_ref, sems.at[1]),
    ]
    for copy in copies:
        copy.start()
    line = lax.broadcasted_iota(jnp.int32, TABLE, 0)
    lane = lax.broadcasted_iota(jnp.int32, TABLE, 1)
    table = jnp.zeros(TABLE, jnp.int32)
    for slot in range(slot_ref.shape[0]):
        table = jnp.where((line == 0) & (lane == slot), slot_ref[slot], table)
    for part in range(mask_ref.shape[0]):
        for nu_block in range(mask_ref.shape[1]):
            table = jnp.where((line == 1 + part) & (lane == nu_block), mask_ref[part, nu_block], table)
    table_ref[...] = table
    copies[0].wait()
    out_ref[0] = chip_half(coeff_held, out_ref.shape[2])
    copies[1].wait()


def next_kernel(next_ref, held_ref, out_ref):
    out_ref[1] = chip_half(next_ref, out_ref.shape[2])


def half_kernel(
    kept_slots, nu_blocks, block, place_ref, own_table, next_table, own_ref, next_ref, *refs
):
    pieces, (out_ref, rows_ref) = refs[:-2], refs[-2:]
    rows, part = pieces[0].shape[1:]
    aux = own_ref.shape[1]
    for index, piece in enumerate(pieces):
        start = pl.multiple_of(place_ref[1 + index] * rows, rows)
        for inner in range(0, rows, block):
            count = min(rows, block)
            nu_block = (start + inner) // block
            for first in range(0, part, block):
                columns = slice(first, first + min(block, part))
                for side, table in enumerate((own_table, next_table)):
                    value = piece[side, inner : inner + count, columns]
                    kept = jnp.where(table[1 + place_ref[0] + first // block, nu_block] != 0, value, jnp.zeros_like(value))
                    rows_ref[side, pl.ds(start + inner, count), columns] = kept
    out_ref[...] = jnp.zeros_like(out_ref)

    def add(table, block_ref, side, slot):
        pair = table[0, slot]

        @pl.when(pair >= 0)
        def _():
            out_rows = pl.ds(pl.multiple_of(pair // nu_blocks * block, block), block)
            nu_rows = rows_ref[side, pl.ds(pl.multiple_of(pair % nu_blocks * block, block), block), :]
            for p in range(aux):
                columns = slice(p * part, (p + 1) * part)
                out_ref[out_rows, columns] += jnp.dot(
                    block_ref[slot, p], nu_rows, preferred_element_type=jnp.float32
                )

    @pl.loop(0, kept_slots)
    def _(slot):
        add(own_table, own_ref, 0, slot)
        add(next_table, next_ref, 1, slot)


def product_kernel(n_left, scale, place_ref, *refs):
    left, right = refs[:n_left], refs[n_left : 2 * n_left]
    out_ref, left_rows, right_rows, tiles, sems = refs[-5:]
    rows = left[0].shape[0]
    for index in range(n_left):
        for base, pieces, held in ((1, left, left_rows), (1 + 2 * n_left, right, right_rows)):
            start = pl.multiple_of(place_ref[base + 2 * index + 1], rows)
            held[place_ref[base + 2 * index], pl.ds(start, rows), :] = pieces[index][...]
    width = tiles.shape[2]
    copies = []
    for tile in range(tiles.shape[0]):
        value = sum(
            lax.dot_general(
                left_rows[chip],
                right_rows[chip, tile * width : (tile + 1) * width, :],
                (((1,), (1,)), ((), ())),
                preferred_element_type=jnp.float32,
            )
            for chip in range(2)
        )
        tiles[tile] = (value * scale).astype(tiles.dtype)
        first = pl.multiple_of(place_ref[0] + tile * width, width)
        copies.append(pltpu.make_async_copy(tiles.at[tile], out_ref.at[:, pl.ds(first, width)], sems.at[tile]))
        copies[-1].start()
    for copy in copies:
        copy.wait()


def exchange(three_index, slot_pair, coeff, occ_mask):
    kept_slots, aux, block = three_index.shape[2:5]
    nu_rows, occ = coeff.shape
    n_row, n_col = lax.axis_size("row"), lax.axis_size("col")
    lay = Layout(n_row, n_col)
    ratio, groups = lay.ratio, lay.groups
    mu_rows, width, part = nu_rows * n_col, aux * occ, occ // 2
    nu_blocks = nu_rows * n_row // block
    row, col = lax.axis_index("row"), lax.axis_index("col")
    plane, side, group, chip = row // ratio, row % ratio, col // 4, col // 2 % 2

    blocks = three_index.reshape(kept_slots, aux, block, block)
    slots, mask = slot_pair.reshape(kept_slots), occ_mask.T
    next_coeff = lay.shift(coeff, col_bits=2)
    shared, blocks, table = pl.pallas_call(
        own_kernel,
        out_shape=(
            jax.ShapeDtypeStruct((2, nu_rows, part), coeff.dtype),
            jax.ShapeDtypeStruct(blocks.shape, blocks.dtype),
            jax.ShapeDtypeStruct(TABLE, jnp.int32),
        ),
        in_specs=[SMEM, SMEM, HBM, HBM],
        out_specs=(VMEM, VMEM, VMEM),
        scratch_shapes=[pltpu.VMEM(coeff.shape, coeff.dtype), pltpu.SemaphoreType.DMA((2,))],
        compiler_params=PARAMS,
    )(slots, mask, coeff, blocks)
    next_table = lay.shift(table, col_bits=2)
    next_blocks = lay.shift(blocks, col_bits=2)
    shared = pl.pallas_call(
        next_kernel,
        out_shape=jax.ShapeDtypeStruct((2, nu_rows, part), coeff.dtype),
        in_specs=[VMEM, VMEM],
        out_specs=VMEM,
        input_output_aliases={1: 0},
        compiler_params=PARAMS,
    )(next_coeff, shared)

    pieces, places = [], []
    for d in range(n_col):
        held = lay.shift(shared, plane_bits=d) if d else shared
        for t in range(ratio):
            here = held
            if t and d == 1:
                here = lay.shift(shared, plane_bits=d, side_bits=t)
            elif t:
                here = lay.shift(held, side_bits=t)
            pieces.append(here)
            places.append((plane ^ d) * ratio + (side ^ t))
    partial = pl.pallas_call(
        functools.partial(half_kernel, kept_slots, nu_blocks, block),
        out_shape=jax.ShapeDtypeStruct((mu_rows, width // 2), jnp.float32),
        in_specs=[SMEM] * 3 + [VMEM] * (2 + len(pieces)),
        out_specs=VMEM,
        scratch_shapes=[pltpu.VMEM((2, nu_blocks * block, part), coeff.dtype)],
        compiler_params=PARAMS,
    )(jnp.stack([chip * part // block] + places), table, next_table, blocks, next_blocks, *pieces)

    total = partial + lay.shift(partial, col_bits=1)
    rows = mu_rows // groups
    if groups > 1:
        mine = [lax.dynamic_slice_in_dim(total, (group ^ e) * rows, rows, 0) for e in range(groups)]
        total = mine[0]
        for e in range(1, groups):
            total = total + lay.shift(mine[e], col_bits=4 * e)
    final = total.astype(jnp.bfloat16)

    pieces = 2 * groups
    left, left_places = [], []
    for e in range(pieces):
        left.append(lay.shift(final, col_bits=2 * e) if e else final)
        left_places += [(col // 2 ^ e) % 2, (col // 2 ^ e) // 2 * rows]
    sources = [lay.permute(final, lambda z, y, w: (w % 2 * pieces + (w // 2 ^ j), y, z)) for j in range(pieces)]
    source_places = []
    for j in range(pieces):
        source_places += [(plane % pieces ^ j) % 2, (plane % pieces ^ j) // 2 * rows]

    out = ()
    columns = math.gcd(mu_rows, 256)
    for t in range(ratio):
        right = [lay.shift(piece, side_bits=t) if t else piece for piece in sources]
        out = pl.pallas_call(
            functools.partial(product_kernel, pieces, 1.0 / math.sqrt(width)),
            out_shape=(jax.ShapeDtypeStruct((mu_rows, ratio * mu_rows), jnp.bfloat16),),
            in_specs=[SMEM] + [VMEM] * (2 * pieces) + [HBM] * len(out),
            out_specs=(HBM,),
            input_output_aliases={1 + 2 * pieces: 0} if out else {},
            scratch_shapes=[
                pltpu.VMEM((2, mu_rows, width // 2), jnp.bfloat16),
                pltpu.VMEM((2, mu_rows, width // 2), jnp.bfloat16),
                pltpu.VMEM((mu_rows // columns, mu_rows, columns), jnp.bfloat16),
                pltpu.SemaphoreType.DMA((mu_rows // columns,)),
            ],
            compiler_params=PARAMS,
        )(jnp.stack([(side ^ t) * mu_rows] + left_places + source_places), *left, *right, *out)
    return out[0]


def solution(mesh):
    return jax.shard_map(
        exchange,
        mesh=mesh,
        in_specs=(
            P("row", "col", None, None, None, None),
            P("row", "col", None),
            P(("col", "row"), None),
            P("col", None),
        ),
        out_specs=P("row", "col"),
        check_vma=False,
    )
```

```python
import functools
import math

import jax
import jax.numpy as jnp
from jax import lax
from jax.experimental import pallas as pl
from jax.experimental.pallas import tpu as pltpu
from jax.sharding import PartitionSpec as P


VMEM = pl.BlockSpec(memory_space=pltpu.VMEM)
HBM = pl.BlockSpec(memory_space=pltpu.HBM)
TABLE = (8, 128)
SMEM = pl.BlockSpec(memory_space=pltpu.SMEM)
PARAMS = pltpu.CompilerParams(vmem_limit_bytes=16 << 20)


class Layout:
    def __init__(self, n_row, n_col):
        self.n_row, self.n_col = n_row, n_col
        self.ratio = n_row // n_col
        self.groups = n_col // 4

    def permute(self, value, target):
        pairs = []
        for row in range(self.n_row):
            for col in range(self.n_col):
                plane, side, place = target(row // self.ratio, row % self.ratio, col)
                pairs.append((row * self.n_col + col, (plane * self.ratio + side) * self.n_col + place))
        return lax.ppermute(value, ("row", "col"), pairs)

    def shift(self, value, plane_bits=0, side_bits=0, col_bits=0):
        return self.permute(value, lambda z, y, w: (z ^ plane_bits, y ^ side_bits, w ^ col_bits))


def chip_half(ref, part):
    chip = lax.axis_index("col") >> 1 & 1
    return ref[:, pl.ds(pl.multiple_of(chip * part, part), part)]


def own_kernel(slot_ref, mask_ref, coeff_ref, blocks_ref, out_ref, held_ref, table_ref, coeff_held, sems):
    copies = [
        pltpu.make_async_copy(coeff_ref, coeff_held, sems.at[0]),
        pltpu.make_async_copy(blocks_ref, held_ref, sems.at[1]),
    ]
    for copy in copies:
        copy.start()
    line = lax.broadcasted_iota(jnp.int32, TABLE, 0)
    lane = lax.broadcasted_iota(jnp.int32, TABLE, 1)
    table = jnp.zeros(TABLE, jnp.int32)
    for slot in range(slot_ref.shape[0]):
        table = jnp.where((line == 0) & (lane == slot), slot_ref[slot], table)
    for part in range(mask_ref.shape[0]):
        for nu_block in range(mask_ref.shape[1]):
            table = jnp.where((line == 1 + part) & (lane == nu_block), mask_ref[part, nu_block], table)
    table_ref[...] = table
    copies[0].wait()
    out_ref[0] = chip_half(coeff_held, out_ref.shape[2])
    copies[1].wait()


def next_kernel(next_ref, held_ref, out_ref):
    out_ref[1] = chip_half(next_ref, out_ref.shape[2])


def half_kernel(
    kept_slots, nu_blocks, block, places, own_table, next_table, own_ref, next_ref, *refs
):
    place_ref = places()
    pieces, (out_ref, rows_ref) = refs[:-2], refs[-2:]
    rows, part = pieces[0].shape[1:]
    aux = own_ref.shape[1]
    for index, piece in enumerate(pieces):
        start = pl.multiple_of(place_ref[1 + index] * rows, rows)
        for inner in range(0, rows, block):
            count = min(rows, block)
            nu_block = (start + inner) // block
            for first in range(0, part, block):
                columns = slice(first, first + min(block, part))
                for side, table in enumerate((own_table, next_table)):
                    value = piece[side, inner : inner + count, columns]
                    kept = jnp.where(table[1 + place_ref[0] + first // block, nu_block] != 0, value, jnp.zeros_like(value))
                    rows_ref[side, pl.ds(start + inner, count), columns] = kept
    out_ref[...] = jnp.zeros_like(out_ref)

    def add(table, block_ref, side, slot):
        pair = table[0, slot]

        @pl.when(pair >= 0)
        def _():
            out_rows = pl.ds(pl.multiple_of(pair // nu_blocks * block, block), block)
            nu_rows = rows_ref[side, pl.ds(pl.multiple_of(pair % nu_blocks * block, block), block), :]
            for p in range(aux):
                columns = slice(p * part, (p + 1) * part)
                out_ref[out_rows, columns] += jnp.dot(
                    block_ref[slot, p], nu_rows, preferred_element_type=jnp.float32
                )

    @pl.loop(0, kept_slots)
    def _(slot):
        add(own_table, own_ref, 0, slot)
        add(next_table, next_ref, 1, slot)


def product_kernel(n_left, scale, places, *refs):
    place_ref = places()
    left, right = refs[:n_left], refs[n_left : 2 * n_left]
    out_ref, left_rows, right_rows, tiles, sems = refs[-5:]
    rows = left[0].shape[0]
    for index in range(n_left):
        for base, pieces, held in ((1, left, left_rows), (1 + 2 * n_left, right, right_rows)):
            start = pl.multiple_of(place_ref[base + 2 * index + 1], rows)
            held[place_ref[base + 2 * index], pl.ds(start, rows), :] = pieces[index][...]
    width = tiles.shape[2]
    copies = []
    for tile in range(tiles.shape[0]):
        value = sum(
            lax.dot_general(
                left_rows[chip],
                right_rows[chip, tile * width : (tile + 1) * width, :],
                (((1,), (1,)), ((), ())),
                preferred_element_type=jnp.float32,
            )
            for chip in range(2)
        )
        tiles[tile] = (value * scale).astype(tiles.dtype)
        first = pl.multiple_of(place_ref[0] + tile * width, width)
        copies.append(pltpu.make_async_copy(tiles.at[tile], out_ref.at[:, pl.ds(first, width)], sems.at[tile]))
        copies[-1].start()
    for copy in copies:
        copy.wait()


def exchange(three_index, slot_pair, coeff, occ_mask):
    kept_slots, aux, block = three_index.shape[2:5]
    nu_rows, occ = coeff.shape
    n_row, n_col = lax.axis_size("row"), lax.axis_size("col")
    lay = Layout(n_row, n_col)
    ratio, groups = lay.ratio, lay.groups
    mu_rows, width, part = nu_rows * n_col, aux * occ, occ // 2
    nu_blocks = nu_rows * n_row // block
    col = lax.axis_index("col")
    group = col // 4

    blocks = three_index.reshape(kept_slots, aux, block, block)
    slots, mask = slot_pair.reshape(kept_slots), occ_mask.T
    next_coeff = lay.shift(coeff, col_bits=2)
    shared, blocks, table = pl.pallas_call(
        own_kernel,
        out_shape=(
            jax.ShapeDtypeStruct((2, nu_rows, part), coeff.dtype),
            jax.ShapeDtypeStruct(blocks.shape, blocks.dtype),
            jax.ShapeDtypeStruct(TABLE, jnp.int32),
        ),
        in_specs=[SMEM, SMEM, HBM, HBM],
        out_specs=(VMEM, VMEM, VMEM),
        scratch_shapes=[pltpu.VMEM(coeff.shape, coeff.dtype), pltpu.SemaphoreType.DMA((2,))],
        compiler_params=PARAMS,
    )(slots, mask, coeff, blocks)
    next_table = lay.shift(table, col_bits=2)
    next_blocks = lay.shift(blocks, col_bits=2)
    shared = pl.pallas_call(
        next_kernel,
        out_shape=jax.ShapeDtypeStruct((2, nu_rows, part), coeff.dtype),
        in_specs=[VMEM, VMEM],
        out_specs=VMEM,
        input_output_aliases={1: 0},
        compiler_params=PARAMS,
    )(next_coeff, shared)

    def gather_places():
        row, col = lax.axis_index("row"), lax.axis_index("col")
        plane, side = row // ratio, row % ratio
        starts = [(plane ^ d) * ratio + (side ^ t) for d in range(n_col) for t in range(ratio)]
        return [(col >> 1 & 1) * part // block] + starts

    pieces = []
    for d in range(n_col):
        held = lay.shift(shared, plane_bits=d) if d else shared
        for t in range(ratio):
            here = held
            if t and d == 1:
                here = lay.shift(shared, plane_bits=d, side_bits=t)
            elif t:
                here = lay.shift(held, side_bits=t)
            pieces.append(here)
    partial = pl.pallas_call(
        functools.partial(half_kernel, kept_slots, nu_blocks, block, gather_places),
        out_shape=jax.ShapeDtypeStruct((mu_rows, width // 2), jnp.float32),
        in_specs=[SMEM] * 2 + [VMEM] * (2 + len(pieces)),
        out_specs=VMEM,
        scratch_shapes=[pltpu.VMEM((2, nu_blocks * block, part), coeff.dtype)],
        compiler_params=PARAMS,
    )(table, next_table, blocks, next_blocks, *pieces)

    total = partial + lay.shift(partial, col_bits=1)
    rows = mu_rows // groups
    if groups > 1:
        mine = [lax.dynamic_slice_in_dim(total, (group ^ e) * rows, rows, 0) for e in range(groups)]
        total = mine[0]
        for e in range(1, groups):
            total = total + lay.shift(mine[e], col_bits=4 * e)
    final = total.astype(jnp.bfloat16)

    pieces = 2 * groups
    left = []
    for e in range(pieces):
        left.append(lay.shift(final, col_bits=2 * e) if e else final)
    sources = [lay.permute(final, lambda z, y, w: (w % 2 * pieces + (w // 2 ^ j), y, z)) for j in range(pieces)]

    def product_places(t):
        row, col = lax.axis_index("row"), lax.axis_index("col")
        plane, side, chips = row // ratio, row % ratio, col >> 1
        starts = [(side ^ t) * mu_rows]
        for e in range(pieces):
            starts += [(chips ^ e) & 1, ((chips ^ e) >> 1) * rows]
        for j in range(pieces):
            source = plane % pieces ^ j
            starts += [source & 1, (source >> 1) * rows]
        return starts

    out = ()
    columns = math.gcd(mu_rows, 256)
    for t in range(ratio):
        right = [lay.shift(piece, side_bits=t) if t else piece for piece in sources]
        out = pl.pallas_call(
            functools.partial(product_kernel, pieces, 1.0 / math.sqrt(width), functools.partial(product_places, t)),
            out_shape=(jax.ShapeDtypeStruct((mu_rows, ratio * mu_rows), jnp.bfloat16),),
            in_specs=[VMEM] * (2 * pieces) + [HBM] * len(out),
            out_specs=(HBM,),
            input_output_aliases={2 * pieces: 0} if out else {},
            scratch_shapes=[
                pltpu.VMEM((2, mu_rows, width // 2), jnp.bfloat16),
                pltpu.VMEM((2, mu_rows, width // 2), jnp.bfloat16),
                pltpu.VMEM((mu_rows // columns, mu_rows, columns), jnp.bfloat16),
                pltpu.SemaphoreType.DMA((mu_rows // columns,)),
            ],
            compiler_params=PARAMS,
        )(*left, *right, *out)
    return out[0]


def solution(mesh):
    return jax.shard_map(
        exchange,
        mesh=mesh,
        in_specs=(
            P("row", "col", None, None, None, None),
            P("row", "col", None),
            P(("col", "row"), None),
            P("col", None),
        ),
        out_specs=P("row", "col"),
        check_vma=False,
    )
```
